32 devices in a mesh: expert: 8 (over z, y), dp: 4 (over x, core).
Axes of the slice: x: 2, y: 2, z: 4, core: 2. Of those that a mesh axis runs over, the one named last changes fastest.
Arguments:
- grad_parts: bfloat16 [4, 8, 3584, 1024], P('dp', 'expert'), may hold values from -6 to 6
- owner_slot: int32 [8], replicated, may hold values from 0 to 7, each once
- slot_expert: int32 [8, 2], replicated, may hold values from 0 to 7, all different within a row
- master: float32 [8, 3584, 1024], P(None, 'expert', 'dp'), may hold values from -1.5 to 1.5
- moment_one: float32 [8, 3584, 1024], P(None, 'expert', 'dp'), may hold values from -2 to 2
- moment_two: float32 [8, 3584, 1024], P(None, 'expert', 'dp'), may hold values from 0.01 to 1
- ema_weights: float32 [8, 3584, 1024], P(None, 'expert', 'dp'), may hold values from -1.5 to 1.5
Outputs:
- master_out: float32 [8, 3584, 1024], P(None, 'expert', 'dp')
- moment_one_out: float32 [8, 3584, 1024], P(None, 'expert', 'dp')
- moment_two_out: float32 [8, 3584, 1024], P(None, 'expert', 'dp')
- ema_out: float32 [8, 3584, 1024], P(None, 'expert', 'dp')
- replicas: bfloat16 [16, 3584, 1024], P('expert', None, 'dp')
The draws below stay inside these ranges and needn't reach their ends.
Inputs may be any that keep to these rules, and one draw needn't show every extreme that they name: `owner_slot`: a permutation of the 8 experts; position k belongs to expert-axis index k. `slot_expert`: each row names 2 different experts, and every expert is named by some row.
All inputs are finite; a program needn't handle non-finite values.
Results may differ from the reference program's by a relative error of at most 0.009.
Values may be sent and summed in bfloat16 or wider, within the bound.
A program may use at most 128 MiB of HBM per device.

```python
import math
import jax
import jax.numpy as jnp
from jax import lax

ROWS = 3584
HIDDEN_SIZE = 1024
SLOTS = 2
STEP = 10
EXPERTS = 8
N_EXPERT = 8
N_DP = 4


def spiked(result, own_key, source, target, parts, factor):
    def block_of(axis_at):
        return (jnp.arange(result.shape[axis_at]) // (result.shape[axis_at] // parts)).reshape((-1,) + (1,) * (result.ndim - 1 - axis_at))

    near = jax.random.permutation(own_key, parts)[block_of(target)]
    second = (block_of(target) + parts // 2) % parts
    return jnp.where((block_of(source) == near) | (block_of(source) == second), factor * result, result)


def shard_levels(rng, dims, pieces, least, high):
    def one(position, shards_of):
        heights = jax.random.uniform(jax.random.fold_in(jax.random.fold_in(rng, 6), position), (shards_of,), jnp.float32, least / len(pieces), high / len(pieces))
        return jnp.repeat(jnp.exp(heights), dims[position] // shards_of).reshape((-1,) + (1,) * (len(dims) - position - 1))

    factor_of = one(*pieces[0])
    for cut in pieces[1:]:
        factor_of = factor_of * one(*cut)
    return factor_of


def choose_distinct(rng, rows, count, top, lift):
    ranking = jax.random.permutation(jax.random.fold_in(rng, 1), count)
    pull = ranking
    for power in range(3):
        pull = pull * pull // count
    pull = pull * lift // count
    tickets = jax.random.randint(jax.random.fold_in(rng, 2), (rows, count), 0, 4096) + pull
    fixed_rows = jax.random.permutation(jax.random.fold_in(rng, 3), rows)[jnp.arange(count) % rows]
    tickets = jnp.where(jnp.arange(rows)[:, None] == fixed_rows[None, :], 1 << 14, tickets)
    priority = tickets * count + jnp.arange(count)
    return lax.top_k(priority.astype(jnp.int32), top)[1].astype(jnp.int32)


def noise(stream_key, dims, scale, most, split=(), kind=jnp.bfloat16):
    drawn = jax.random.normal(stream_key, dims, jnp.float32) * scale
    if len(split) > 0:
        drawn = shard_levels(stream_key, dims, split, -0.22, 0.18) * drawn
    return jnp.clip(drawn, min=-most, max=most).astype(kind)


def gaussian_with(own_key, shape, width, limit, split, heavy, kind=jnp.bfloat16):
    result = width * jax.random.normal(own_key, shape, jnp.float32)
    if split:
        result = result * shard_levels(own_key, shape, split, -0.22, 0.18)
    return jnp.clip(spiked(result, jax.random.fold_in(own_key, 3), *heavy), -limit, limit).astype(kind)


def setup_inputs(seed: int = 0) -> dict:
    seeds = jax.random.split(jax.random.key(seed), 8)
    grad_parts = gaussian_with(seeds[0], (N_DP, EXPERTS, ROWS, HIDDEN_SIZE), 1.0, 6.0, ((0, 4), (1, 8)), (0, 3, 4, 2.0))
    owner_slot = jax.random.permutation(seeds[1], EXPERTS).astype(jnp.int32)
    slot_expert = choose_distinct(seeds[2], N_EXPERT, EXPERTS, SLOTS, 4096)
    master = noise(seeds[3], (EXPERTS, ROWS, HIDDEN_SIZE), 0.25, 1.5, ((1, 8), (2, 4)), jnp.float32)
    moment_one = noise(seeds[4], (EXPERTS, ROWS, HIDDEN_SIZE), 0.3, 2.0, ((1, 8), (2, 4)), jnp.float32)
    moment_two = jnp.clip(jnp.exp(math.log(1.0) - 4.6051702 * jax.random.uniform(seeds[5], (EXPERTS, ROWS, HIDDEN_SIZE), jnp.float32) ** shard_levels(seeds[5], (EXPERTS, ROWS, HIDDEN_SIZE), ((1, 8), (2, 4)), -0.2, 0.2)), 0.01, 1.0)
    ema_weights = noise(seeds[6], (EXPERTS, ROWS, HIDDEN_SIZE), 0.25, 1.5, ((1, 8), (2, 4)), jnp.float32)
    return {"grad_parts": grad_parts, "owner_slot": owner_slot, "slot_expert": slot_expert, "master": master, "moment_one": moment_one, "moment_two": moment_two, "ema_weights": ema_weights}


beta_one = 0.9
beta_two = 0.999
adam_eps = 1e-08
learn_rate = 0.05
decay_rate = 0.1
ema_decay = 0.99

def reference(grad_parts, owner_slot, slot_expert, master, moment_one, moment_two, ema_weights):
    summed = grad_parts[0].astype(jnp.float32)
    for copy_index in range(1, N_DP):
        summed = summed + grad_parts[copy_index].astype(jnp.float32)
    gradient = jnp.take(summed, owner_slot, axis=0)
    correct_one = 1.0 - beta_one ** STEP
    correct_two = 1.0 - beta_two ** STEP
    moment_one_out = beta_one * moment_one + (1.0 - beta_one) * gradient
    moment_two_out = beta_two * moment_two + (1.0 - beta_two) * gradient * gradient
    update = moment_one_out / correct_one / (jnp.sqrt(moment_two_out / correct_two) + adam_eps)
    master_out = master - learn_rate * (update + decay_rate * master)
    ema_out = ema_decay * ema_weights + (1.0 - ema_decay) * master_out
    replicas = jnp.take(master_out, slot_expert.reshape(-1), axis=0).astype(jnp.bfloat16)
    return (master_out, moment_one_out, moment_two_out, ema_out, replicas)
```

```python
import functools

import jax
import jax.numpy as jnp
from jax import lax
from jax.experimental import pallas as pl
from jax.experimental.pallas import tpu as pltpu
from jax.sharding import PartitionSpec as P

STEP = 10


beta_one = 0.9
beta_two = 0.999
adam_eps = 1e-08
learn_rate = 0.05
decay_rate = 0.1
ema_decay = 0.99

MESH = pl.DeviceIdType.MESH
CORES = 2
VMEM_LIMIT = 60 * 1024 * 1024


def row_tile(rows, most):
    return max(t for t in range(16, most + 1, 16) if rows % t == 0)


def reduce_kernel(n_e, n_dp, grad, out, own, got, part, peer, done,
                  load_sem, pair_send, pair_recv, part_send, part_recv, out_send, out_recv, self_sem):
    chips = n_dp // CORES
    rows = grad.shape[0] // n_e
    cols = grad.shape[1] // n_dp
    e = lax.axis_index("expert")
    d = lax.axis_index("dp")
    chip, core = d // CORES, d % CORES
    other = 1 - core
    half = n_e // 2
    side, place = e // half, e % half

    barrier = pltpu.get_barrier_semaphore()
    for r in range(1, n_dp):
        pl.semaphore_signal(barrier, inc=1, device_id=(e, lax.rem(d + r, n_dp)), device_id_type=MESH)
    for r in range(1, n_e):
        pl.semaphore_signal(barrier, inc=1, device_id=(lax.rem(e + r, n_e), d), device_id_type=MESH)

    def holder(k):
        if k < half:
            return (1 - side) * half + lax.rem(place + k, half)
        return side * half + lax.rem(place + (k - half + 1), half)

    def block(k, chip_of, core_of):
        first = pl.multiple_of(holder(k) * rows, rows)
        column = pl.multiple_of((chip_of * CORES + core_of) * cols, cols)
        return grad.at[pl.ds(first, rows), pl.ds(column, cols)]

    def chip_at(r):
        return lax.rem(chip + 1 + r, chips)

    loads, pairs = {}, {}
    for k in range(n_e):
        for r in range(chips):
            loads[k, r] = pltpu.make_async_copy(block(k, chip_at(r), core), own.at[k, r], load_sem.at[k, r])
            loads[k, r].start()
    pl.semaphore_wait(barrier, n_dp - 1 + n_e - 1)
    for k in range(n_e):
        for r in range(chips):
            pairs[k, r] = pltpu.make_async_remote_copy(
                src_ref=block(k, chip_at(r), other), dst_ref=got.at[k, r],
                send_sem=pair_send.at[k, r], recv_sem=pair_recv.at[k, r],
                device_id=(e, chip * CORES + other), device_id_type=MESH)
            pairs[k, r].start()

    tile = row_tile(rows, 64)
    parts, outs = {}, {}

    def to_chips(k):
        for r in range(chips - 1):
            loads[k, r].wait()
            pairs[k, r].wait_recv()

            @pl.loop(0, rows // tile)
            def _(i):
                at = pl.ds(pl.multiple_of(i * tile, tile), tile)
                total = own[k, r, at, :].astype(jnp.float32) + got[k, r, at, :].astype(jnp.float32)
                part[k, r, at, :] = total.astype(jnp.bfloat16)

            parts[k, r] = pltpu.make_async_remote_copy(
                src_ref=part.at[k, r], dst_ref=peer.at[k, r],
                send_sem=part_send.at[k, r], recv_sem=part_recv.at[k, r],
                device_id=(e, chip_at(r) * CORES + core), device_id_type=MESH)
            parts[k, r].start()

    def to_holder(k):
        r_own = chips - 1
        loads[k, r_own].wait()
        pairs[k, r_own].wait_recv()
        for r in range(chips - 1):
            parts[k, r].wait_recv()

        @pl.loop(0, rows // tile)
        def _(i):
            at = pl.ds(pl.multiple_of(i * tile, tile), tile)
            total = own[k, r_own, at, :].astype(jnp.float32) + got[k, r_own, at, :].astype(jnp.float32)
            for r in range(chips - 1):
                total = total + peer[k, r, at, :].astype(jnp.float32)
            done[k, at, :] = total.astype(jnp.bfloat16)

        if k < n_e - 1:
            outs[k] = pltpu.make_async_remote_copy(
                src_ref=done.at[k], dst_ref=out.at[e],
                send_sem=out_send.at[k], recv_sem=out_recv.at[k],
                device_id=(holder(k), d), device_id_type=MESH)
        else:
            outs[k] = pltpu.make_async_copy(done.at[k], out.at[e], self_sem)
        outs[k].start()

    ahead = min(2, n_e)
    for k in range(ahead):
        to_chips(k)
    for k in range(n_e):
        if k + ahead < n_e:
            to_chips(k + ahead)
        to_holder(k)

    for k in range(n_e):
        for r in range(chips):
            pairs[k, r].wait_send()
        for r in range(chips - 1):
            parts[k, r].wait_send()
        outs[k].wait()


def owned_rows(n_e, n_dp, grad):
    rows, cols = grad.shape[0] // n_e, grad.shape[1] // n_dp
    chips = n_dp // CORES
    dma = pltpu.SemaphoreType.DMA
    sent = grad.size * 2
    return pl.pallas_call(
        functools.partial(reduce_kernel, n_e, n_dp),
        out_shape=jax.ShapeDtypeStruct((n_e, rows, cols), jnp.bfloat16),
        in_specs=[pl.BlockSpec(memory_space=pl.ANY)],
        out_specs=pl.BlockSpec(memory_space=pl.ANY),
        scratch_shapes=[
            pltpu.VMEM((n_e, chips, rows, cols), jnp.bfloat16),
            pltpu.VMEM((n_e, chips, rows, cols), jnp.bfloat16),
            pltpu.VMEM((n_e, chips - 1, rows, cols), jnp.bfloat16),
            pltpu.VMEM((n_e, chips - 1, rows, cols), jnp.bfloat16),
            pltpu.VMEM((n_e, rows, cols), jnp.bfloat16),
            dma((n_e, chips)),
            dma((n_e, chips)),
            dma((n_e, chips)),
            dma((n_e, chips - 1)),
            dma((n_e, chips - 1)),
            dma((n_e,)),
            dma((n_e,)),
            dma(()),
        ],
        compiler_params=pltpu.CompilerParams(
            collective_id=0, has_side_effects=True, vmem_limit_bytes=VMEM_LIMIT),
        cost_estimate=pl.CostEstimate(flops=2 * grad.size, bytes_accessed=2 * sent, transcendentals=0),
        name="reduce_rows",
    )(grad)


def adam(gradient, master, one, two):
    scale_one = 1.0 / (1.0 - beta_one**STEP)
    scale_two = 1.0 / (1.0 - beta_two**STEP)
    one_out = beta_one * one + (1.0 - beta_one) * gradient
    two_out = beta_two * two + (1.0 - beta_two) * gradient * gradient
    update = one_out * scale_one / (jnp.sqrt(two_out * scale_two) + adam_eps)
    return master - learn_rate * (update + decay_rate * master), one_out, two_out


def outgoing_kernel(owner, slots, rows_ref, master, one, two, out, held):
    n_e, tile, _ = master.shape
    step = row_tile(tile, 32)

    @pl.loop(0, n_e)
    def _(x):
        @pl.loop(0, tile // step)
        def _(i):
            at = pl.ds(pl.multiple_of(i * step, step), step)
            gradient = rows_ref[owner[x], at, :].astype(jnp.float32)
            held[x, at, :] = adam(gradient, master[x, at, :], one[x, at, :], two[x, at, :])[0].astype(jnp.bfloat16)

    @pl.loop(0, out.shape[0])
    def _(s):
        out[s] = held[slots[s]]


def outgoing_rows(owner_rows, owner_slot, slots, master, one, two):
    n_e, rows, cols = master.shape
    tile = row_tile(rows, 112)
    spec = pl.BlockSpec((n_e, tile, cols), lambda i, *_: (0, i, 0))
    return pl.pallas_call(
        outgoing_kernel,
        out_shape=jax.ShapeDtypeStruct((slots.shape[0], rows, cols), jnp.bfloat16),
        grid_spec=pltpu.PrefetchScalarGridSpec(
            num_scalar_prefetch=2, grid=(rows // tile,),
            in_specs=[spec] * 4,
            out_specs=pl.BlockSpec((slots.shape[0], tile, cols), lambda i, *_: (0, i, 0)),
            scratch_shapes=[pltpu.VMEM((n_e, tile, cols), jnp.bfloat16)]),
        compiler_params=pltpu.CompilerParams(vmem_limit_bytes=VMEM_LIMIT),
        cost_estimate=pl.CostEstimate(
            flops=16 * master.size, bytes_accessed=18 * master.size, transcendentals=2 * master.size),
        name="outgoing_rows",
    )(owner_slot, slots, owner_rows, master, one, two)


def update_kernel(owner, rows_ref, master, one, two, ema, master_out, one_out, two_out, ema_out):
    n_e, tile, _ = master.shape
    step = row_tile(tile, 32)

    @pl.loop(0, n_e)
    def _(x):
        @pl.loop(0, tile // step)
        def _(i):
            at = pl.ds(pl.multiple_of(i * step, step), step)
            gradient = rows_ref[owner[x], at, :].astype(jnp.float32)
            new, first, second = adam(gradient, master[x, at, :], one[x, at, :], two[x, at, :])
            master_out[x, at, :] = new
            one_out[x, at, :] = first
            two_out[x, at, :] = second
            ema_out[x, at, :] = ema_decay * ema[x, at, :] + (1.0 - ema_decay) * new


def updated_state(owner_rows, owner_slot, master, one, two, ema):
    n_e, rows, cols = master.shape
    tile = row_tile(rows, 112)
    spec = pl.BlockSpec((n_e, tile, cols), lambda i, *_: (0, i, 0))
    return pl.pallas_call(
        update_kernel,
        out_shape=[jax.ShapeDtypeStruct(master.shape, jnp.float32)] * 4,
        grid_spec=pltpu.PrefetchScalarGridSpec(
            num_scalar_prefetch=1, grid=(rows // tile,),
            in_specs=[spec] * 5, out_specs=[spec] * 4),
        compiler_params=pltpu.CompilerParams(vmem_limit_bytes=VMEM_LIMIT),
        cost_estimate=pl.CostEstimate(
            flops=20 * master.size, bytes_accessed=34 * master.size, transcendentals=2 * master.size),
        name="updated_state",
    )(owner_slot, owner_rows, master, one, two, ema)


def per_device(n_e, n_dp, grad_parts, owner_slot, slot_expert, master, moment_one, moment_two, ema_weights):
    owner_rows = owned_rows(n_e, n_dp, grad_parts[0, 0])
    outgoing = outgoing_rows(owner_rows, owner_slot, slot_expert.reshape(-1), master, moment_one, moment_two)
    replicas = lax.all_to_all(outgoing, "expert", split_axis=0, concat_axis=1, tiled=True)
    master_out, moment_one_out, moment_two_out, ema_out = updated_state(
        owner_rows, owner_slot, master, moment_one, moment_two, ema_weights)
    return (master_out, moment_one_out, moment_two_out, ema_out, replicas)


def solution(mesh):
    placed = (
        P("dp", "expert", None, None),
        P(),
        P(),
        P(None, "expert", "dp"),
        P(None, "expert", "dp"),
        P(None, "expert", "dp"),
        P(None, "expert", "dp"),
    )
    return jax.shard_map(
        functools.partial(per_device, mesh.shape["expert"], mesh.shape["dp"]),
        mesh=mesh,
        in_specs=placed,
        out_specs=(
            P(None, "expert", "dp"),
            P(None, "expert", "dp"),
            P(None, "expert", "dp"),
            P(None, "expert", "dp"),
            P("expert", None, "dp"),
        ),
        check_vma=False,
    )
```

```python
import functools

import jax
import jax.numpy as jnp
from jax import lax
from jax.experimental import pallas as pl
from jax.experimental.pallas import tpu as pltpu
from jax.sharding import PartitionSpec as P

STEP = 10


beta_one = 0.9
beta_two = 0.999
adam_eps = 1e-08
learn_rate = 0.05
decay_rate = 0.1
ema_decay = 0.99

MESH = pl.DeviceIdType.MESH
CORES = 2
VMEM_LIMIT = 60 * 1024 * 1024
CHUNKS = 2


def row_tile(rows, most):
    return max(t for t in range(16, most + 1, 16) if rows % t == 0)


def adam(gradient, master, one, two):
    scale_one = 1.0 / (1.0 - beta_one**STEP)
    scale_two = 1.0 / (1.0 - beta_two**STEP)
    one_out = beta_one * one + (1.0 - beta_one) * gradient
    two_out = beta_two * two + (1.0 - beta_two) * gradient * gradient
    update = one_out * scale_one / (jnp.sqrt(two_out * scale_two) + adam_eps)
    return master - learn_rate * (update + decay_rate * master), one_out, two_out


def exchange_kernel(n_e, n_dp, chunks, owner, slots, grad, master, one, two, replicas, rows_out, *refs):
    gathered, slotted = refs[:chunks], refs[chunks:2 * chunks]
    (own, got, part, peer, done, held, master_in, one_in, two_in,
     load_sem, pair_send, pair_recv, part_send, part_recv, out_send, out_recv,
     state_sem, rows_sem, slot_send, slot_recv, self_sem) = refs[2 * chunks:]
    chips = n_dp // CORES
    rows = grad.shape[0] // n_e
    cols = grad.shape[1] // n_dp
    size = rows // chunks
    e = lax.axis_index("expert")
    d = lax.axis_index("dp")
    chip, core = d // CORES, d % CORES
    other = 1 - core
    half = n_e // 2
    side, place = e // half, e % half
    tile = row_tile(size, 32)
    steps = chunks * n_e

    barrier = pltpu.get_barrier_semaphore()
    for r in range(1, n_dp):
        pl.semaphore_signal(barrier, inc=1, device_id=(e, lax.rem(d + r, n_dp)), device_id_type=MESH)
    for r in range(1, n_e):
        pl.semaphore_signal(barrier, inc=1, device_id=(lax.rem(e + r, n_e), d), device_id_type=MESH)

    def holder(k):
        if k < half:
            return (1 - side) * half + lax.rem(place + k, half)
        return side * half + lax.rem(place + (k - half + 1), half)

    def block(j, chip_of, core_of):
        first = pl.multiple_of(holder(j % n_e) * rows + (j // n_e) * size, size)
        column = pl.multiple_of((chip_of * CORES + core_of) * cols, cols)
        return grad.at[pl.ds(first, size), pl.ds(column, cols)]

    def chip_at(r):
        return lax.rem(chip + 1 + r, chips)

    loads, pairs = {}, {}
    for j in range(steps):
        for r in range(chips):
            loads[j, r] = pltpu.make_async_copy(block(j, chip_at(r), core), own.at[j, r], load_sem.at[j, r])
            loads[j, r].start()
    pl.semaphore_wait(barrier, n_dp - 1 + n_e - 1)
    for j in range(steps):
        for r in range(chips):
            pairs[j, r] = pltpu.make_async_remote_copy(
                src_ref=block(j, chip_at(r), other), dst_ref=got.at[j, r],
                send_sem=pair_send.at[j, r], recv_sem=pair_recv.at[j, r],
                device_id=(e, chip * CORES + other), device_id_type=MESH)
            pairs[j, r].start()
    states = [pltpu.make_async_copy(src, dst, state_sem.at[i]) for i, (src, dst) in
              enumerate(((master, master_in), (one, one_in), (two, two_in)))]
    for copy in states:
        copy.start()

    parts, outs, sends, kept = {}, {}, {}, {}

    def to_chips(j):
        for r in range(chips - 1):
            loads[j, r].wait()
            pairs[j, r].wait_recv()

            @pl.loop(0, size // tile)
            def _(i):
                at = pl.ds(pl.multiple_of(i * tile, tile), tile)
                total = own[j, r, at, :].astype(jnp.float32) + got[j, r, at, :].astype(jnp.float32)
                part[j, r, at, :] = total.astype(jnp.bfloat16)

            parts[j, r] = pltpu.make_async_remote_copy(
                src_ref=part.at[j, r], dst_ref=peer.at[j, r],
                send_sem=part_send.at[j, r], recv_sem=part_recv.at[j, r],
                device_id=(e, chip_at(r) * CORES + core), device_id_type=MESH)
            parts[j, r].start()

    def to_holder(j):
        c, k = j // n_e, j % n_e
        away = k < n_e - 1
        r_own = chips - 1
        loads[j, r_own].wait()
        pairs[j, r_own].wait_recv()
        for r in range(chips - 1):
            parts[j, r].wait_recv()

        @pl.loop(0, size // tile)
        def _(i):
            at = pl.ds(pl.multiple_of(i * tile, tile), tile)
            total = own[j, r_own, at, :].astype(jnp.float32) + got[j, r_own, at, :].astype(jnp.float32)
            for r in range(chips - 1):
                total = total + peer[j, r, at, :].astype(jnp.float32)
            if away:
                done[j, at, :] = total.astype(jnp.bfloat16)
            else:
                gathered[c][e, at, :] = total.astype(jnp.bfloat16)

        if away:
            outs[j] = pltpu.make_async_remote_copy(
                src_ref=done.at[j], dst_ref=gathered[c].at[e],
                send_sem=out_send.at[j], recv_sem=out_recv.at[j],
                device_id=(holder(k), d), device_id_type=MESH)
            outs[j].start()

    def to_hosts(c):
        for k in range(n_e - 1):
            outs[c * n_e + k].wait_recv()
        kept[c] = pltpu.make_async_copy(
            gathered[c], rows_out.at[:, pl.ds(c * size, size), :], rows_sem.at[c])
        kept[c].start()

        @pl.loop(0, n_e)
        def _(x):
            position = owner[x]

            @pl.loop(0, size // tile)
            def _(i):
                at = pl.ds(pl.multiple_of(i * tile, tile), tile)
                there = pl.ds(pl.multiple_of(c * size + i * tile, tile), tile)
                gradient = gathered[c][position, at, :].astype(jnp.float32)
                new = adam(gradient, master_in[x, there, :], one_in[x, there, :], two_in[x, there, :])[0]
                held[x, at, :] = new.astype(jnp.bfloat16)

        width = replicas.shape[0]
        for k in range(n_e):
            host = holder(k)
            for s in range(width):
                wanted = slots[host * width + s]

                @pl.loop(0, size // tile)
                def _(i):
                    at = pl.ds(pl.multiple_of(i * tile, tile), tile)
                    slotted[c][k, s, at, :] = held[wanted, at, :]

            first = pl.multiple_of(e * rows + c * size, size)
            target = replicas.at[:, pl.ds(first, size), :]
            j = c * n_e + k
            if k < n_e - 1:
                sends[j] = pltpu.make_async_remote_copy(
                    src_ref=slotted[c].at[k], dst_ref=target,
                    send_sem=slot_send.at[j], recv_sem=slot_recv.at[j],
                    device_id=(host, d), device_id_type=MESH)
            else:
                sends[j] = pltpu.make_async_copy(slotted[c].at[k], target, self_sem.at[c])
            sends[j].start()

    ahead = min(3, steps)
    for j in range(ahead):
        to_chips(j)
    for j in range(steps):
        if j + ahead < steps:
            to_chips(j + ahead)
        to_holder(j)

    for copy in states:
        copy.wait()
    for c in range(chunks):
        to_hosts(c)

    for j in range(steps):
        for r in range(chips):
            pairs[j, r].wait_send()
        for r in range(chips - 1):
            parts[j, r].wait_send()
        if j in outs:
            outs[j].wait_send()
    for c in range(chunks):
        kept[c].wait()
    for j in range(steps):
        sends[j].wait()


def exchanged(n_e, n_dp, grad, owner_slot, slot_expert, master, one, two):
    rows, cols = grad.shape[0] // n_e, grad.shape[1] // n_dp
    chips = n_dp // CORES
    width = slot_expert.shape[1]
    chunks = CHUNKS
    size = rows // chunks
    steps = chunks * n_e
    dma = pltpu.SemaphoreType.DMA
    half = jnp.bfloat16
    hbm = pl.BlockSpec(memory_space=pl.ANY)
    smem = pl.BlockSpec(memory_space=pltpu.SMEM)
    return pl.pallas_call(
        functools.partial(exchange_kernel, n_e, n_dp, chunks),
        out_shape=[
            jax.ShapeDtypeStruct((width, n_e * rows, cols), half),
            jax.ShapeDtypeStruct((n_e, rows, cols), half),
        ],
        in_specs=[smem, smem, hbm, hbm, hbm, hbm],
        out_specs=[hbm, hbm],
        scratch_shapes=[pltpu.VMEM((n_e, size, cols), half)] * chunks
        + [pltpu.VMEM((n_e, width, size, cols), half)] * chunks
        + [
            pltpu.VMEM((steps, chips, size, cols), half),
            pltpu.VMEM((steps, chips, size, cols), half),
            pltpu.VMEM((steps, chips - 1, size, cols), half),
            pltpu.VMEM((steps, chips - 1, size, cols), half),
            pltpu.VMEM((steps, size, cols), half),
            pltpu.VMEM((n_e, size, cols), half),
            pltpu.VMEM((n_e, rows, cols), jnp.float32),
            pltpu.VMEM((n_e, rows, cols), jnp.float32),
            pltpu.VMEM((n_e, rows, cols), jnp.float32),
            dma((steps, chips)),
            dma((steps, chips)),
            dma((steps, chips)),
            dma((steps, chips - 1)),
            dma((steps, chips - 1)),
            dma((steps,)),
            dma((steps,)),
            dma((3,)),
            dma((chunks,)),
            dma((steps,)),
            dma((steps,)),
            dma((chunks,)),
        ],
        compiler_params=pltpu.CompilerParams(
            collective_id=0, has_side_effects=True, vmem_limit_bytes=VMEM_LIMIT),
        name="exchange",
    )(owner_slot, slot_expert.reshape(-1), grad, master, one, two)


def update_kernel(owner, rows_ref, replicas, master, one, two, ema,
                  replicas_out, master_out, one_out, two_out, ema_out):
    n_e, tile, _ = master.shape
    step = row_tile(tile, 32)
    replicas_out[...] = replicas[...]

    @pl.loop(0, n_e)
    def _(x):
        @pl.loop(0, tile // step)
        def _(i):
            at = pl.ds(pl.multiple_of(i * step, step), step)
            gradient = rows_ref[owner[x], at, :].astype(jnp.float32)
            new, first, second = adam(gradient, master[x, at, :], one[x, at, :], two[x, at, :])
            master_out[x, at, :] = new
            one_out[x, at, :] = first
            two_out[x, at, :] = second
            ema_out[x, at, :] = ema_decay * ema[x, at, :] + (1.0 - ema_decay) * new


def updated_state(owner_rows, replicas, owner_slot, master, one, two, ema):
    n_e, rows, cols = master.shape
    tile = row_tile(rows, 64)
    spec = pl.BlockSpec((n_e, tile, cols), lambda i, *_: (0, i, 0))
    width, height, _ = replicas.shape
    slot_spec = pl.BlockSpec((width, height * tile // rows, cols), lambda i, *_: (0, i, 0))
    return pl.pallas_call(
        update_kernel,
        out_shape=[jax.ShapeDtypeStruct(replicas.shape, replicas.dtype)]
        + [jax.ShapeDtypeStruct(master.shape, jnp.float32)] * 4,
        grid_spec=pltpu.PrefetchScalarGridSpec(
            num_scalar_prefetch=1, grid=(rows // tile,),
            in_specs=[spec, slot_spec] + [spec] * 4, out_specs=[slot_spec] + [spec] * 4),
        compiler_params=pltpu.CompilerParams(vmem_limit_bytes=VMEM_LIMIT),
        name="updated_state",
    )(owner_slot, owner_rows, replicas, master, one, two, ema)


def per_device(n_e, n_dp, grad_parts, owner_slot, slot_expert, master, moment_one, moment_two, ema_weights):
    arrived, owner_rows = exchanged(
        n_e, n_dp, grad_parts[0, 0], owner_slot, slot_expert, master, moment_one, moment_two)
    replicas, master_out, moment_one_out, moment_two_out, ema_out = updated_state(
        owner_rows, arrived, owner_slot, master, moment_one, moment_two, ema_weights)
    return (master_out, moment_one_out, moment_two_out, ema_out, replicas)


def solution(mesh):
    placed = (
        P("dp", "expert", None, None),
        P(),
        P(),
        P(None, "expert", "dp"),
        P(None, "expert", "dp"),
        P(None, "expert", "dp"),
        P(None, "expert", "dp"),
    )
    return jax.shard_map(
        functools.partial(per_device, mesh.shape["expert"], mesh.shape["dp"]),
        mesh=mesh,
        in_specs=placed,
        out_specs=(
            P(None, "expert", "dp"),
            P(None, "expert", "dp"),
            P(None, "expert", "dp"),
            P(None, "expert", "dp"),
            P("expert", None, "dp"),
        ),
        check_vma=False,
    )
```

```python
import functools

import jax
import jax.numpy as jnp
from jax import lax
from jax.experimental import pallas as pl
from jax.experimental.pallas import tpu as pltpu
from jax.sharding import PartitionSpec as P

STEP = 10


beta_one = 0.9
beta_two = 0.999
adam_eps = 1e-08
learn_rate = 0.05
decay_rate = 0.1
ema_decay = 0.99

MESH = pl.DeviceIdType.MESH
CORES = 2
VMEM_LIMIT = 40 * 1024 * 1024
CHUNKS = 2


def row_tile(rows, most):
    return max(t for t in range(16, most + 1, 16) if rows % t == 0)


def adam(gradient, master, one, two):
    scale_one = 1.0 / (1.0 - beta_one**STEP)
    scale_two = 1.0 / (1.0 - beta_two**STEP)
    one_out = beta_one * one + (1.0 - beta_one) * gradient
    two_out = beta_two * two + (1.0 - beta_two) * gradient * gradient
    update = one_out * scale_one / (jnp.sqrt(two_out * scale_two) + adam_eps)
    return master - learn_rate * (update + decay_rate * master), one_out, two_out


def exchange_kernel(n_e, n_dp, chunks, owner, slots, grad, master, one, two, ema,
                    master_out, one_out, two_out, ema_out, replicas, *refs):
    gathered, slotted = refs[:chunks], refs[chunks:2 * chunks]
    (own, got, part, peer, done, held,
     load_sem, pair_send, pair_recv, part_send, part_recv, out_send, out_recv,
     state_sem, slot_send, slot_recv, self_sem) = refs[2 * chunks:]
    chips = n_dp // CORES
    rows = grad.shape[0] // n_e
    cols = grad.shape[1] // n_dp
    size = rows // chunks
    e = lax.axis_index("expert")
    d = lax.axis_index("dp")
    chip, core = d // CORES, d % CORES
    other = 1 - core
    half = n_e // 2
    side, place = e // half, e % half
    tile = row_tile(size, 32)
    steps = chunks * n_e

    barrier = pltpu.get_barrier_semaphore()
    for r in range(1, n_dp):
        pl.semaphore_signal(barrier, inc=1, device_id=(e, lax.rem(d + r, n_dp)), device_id_type=MESH)
    for r in range(1, n_e):
        pl.semaphore_signal(barrier, inc=1, device_id=(lax.rem(e + r, n_e), d), device_id_type=MESH)

    def holder(k):
        if k < half:
            return (1 - side) * half + lax.rem(place + k, half)
        return side * half + lax.rem(place + (k - half + 1), half)

    def block(j, chip_of, core_of):
        first = pl.multiple_of(holder(j % n_e) * rows + (j // n_e) * size, size)
        column = pl.multiple_of((chip_of * CORES + core_of) * cols, cols)
        return grad.at[pl.ds(first, size), pl.ds(column, cols)]

    def chip_at(r):
        return lax.rem(chip + 1 + r, chips)

    loads, pairs = {}, {}
    for j in range(steps):
        for r in range(chips):
            loads[j, r] = pltpu.make_async_copy(block(j, chip_at(r), core), own.at[j, r], load_sem.at[j, r])
            loads[j, r].start()
    pl.semaphore_wait(barrier, n_dp - 1 + n_e - 1)
    for j in range(steps):
        for r in range(chips):
            pairs[j, r] = pltpu.make_async_remote_copy(
                src_ref=block(j, chip_at(r), other), dst_ref=got.at[j, r],
                send_sem=pair_send.at[j, r], recv_sem=pair_recv.at[j, r],
                device_id=(e, chip * CORES + other), device_id_type=MESH)
            pairs[j, r].start()
    states = [pltpu.make_async_copy(src, dst, state_sem.at[i]) for i, (src, dst) in
              enumerate(((master, master_out), (one, one_out), (two, two_out), (ema, ema_out)))]
    for copy in states:
        copy.start()

    parts, outs, sends = {}, {}, {}

    def to_chips(j):
        for r in range(chips - 1):
            loads[j, r].wait()
            pairs[j, r].wait_recv()

            @pl.loop(0, size // tile)
            def _(i):
                at = pl.ds(pl.multiple_of(i * tile, tile), tile)
                total = own[j, r, at, :].astype(jnp.float32) + got[j, r, at, :].astype(jnp.float32)
                part[j, r, at, :] = total.astype(jnp.bfloat16)

            parts[j, r] = pltpu.make_async_remote_copy(
                src_ref=part.at[j, r], dst_ref=peer.at[j, r],
                send_sem=part_send.at[j, r], recv_sem=part_recv.at[j, r],
                device_id=(e, chip_at(r) * CORES + core), device_id_type=MESH)
            parts[j, r].start()

    def to_holder(j):
        c, k = j // n_e, j % n_e
        away = k < n_e - 1
        r_own = chips - 1
        loads[j, r_own].wait()
        pairs[j, r_own].wait_recv()
        for r in range(chips - 1):
            parts[j, r].wait_recv()

        @pl.loop(0, size // tile)
        def _(i):
            at = pl.ds(pl.multiple_of(i * tile, tile), tile)
            total = own[j, r_own, at, :].astype(jnp.float32) + got[j, r_own, at, :].astype(jnp.float32)
            for r in range(chips - 1):
                total = total + peer[j, r, at, :].astype(jnp.float32)
            if away:
                done[j, at, :] = total.astype(jnp.bfloat16)
            else:
                gathered[c][e, at, :] = total.astype(jnp.bfloat16)

        if away:
            outs[j] = pltpu.make_async_remote_copy(
                src_ref=done.at[j], dst_ref=gathered[c].at[e],
                send_sem=out_send.at[j], recv_sem=out_recv.at[j],
                device_id=(holder(k), d), device_id_type=MESH)
            outs[j].start()

    def to_hosts(c):
        for k in range(n_e - 1):
            outs[c * n_e + k].wait_recv()

        @pl.loop(0, n_e)
        def _(x):
            position = owner[x]

            @pl.loop(0, size // tile)
            def _(i):
                at = pl.ds(pl.multiple_of(i * tile, tile), tile)
                there = pl.ds(pl.multiple_of(c * size + i * tile, tile), tile)
                gradient = gathered[c][position, at, :].astype(jnp.float32)
                new, first, second = adam(
                    gradient, master_out[x, there, :], one_out[x, there, :], two_out[x, there, :])
                held[x, at, :] = new.astype(jnp.bfloat16)
                master_out[x, there, :] = new
                one_out[x, there, :] = first
                two_out[x, there, :] = second

        width = replicas.shape[0]
        for k in range(n_e):
            host = holder(k)
            for s in range(width):
                wanted = slots[host * width + s]

                @pl.loop(0, size // tile)
                def _(i):
                    at = pl.ds(pl.multiple_of(i * tile, tile), tile)
                    slotted[c][k, s, at, :] = held[wanted, at, :]

            first = pl.multiple_of(e * rows + c * size, size)
            target = replicas.at[:, pl.ds(first, size), :]
            j = c * n_e + k
            if k < n_e - 1:
                sends[j] = pltpu.make_async_remote_copy(
                    src_ref=slotted[c].at[k], dst_ref=target,
                    send_sem=slot_send.at[j], recv_sem=slot_recv.at[j],
                    device_id=(host, d), device_id_type=MESH)
            else:
                sends[j] = pltpu.make_async_copy(slotted[c].at[k], target, self_sem.at[c])
            sends[j].start()

        @pl.loop(0, n_e)
        def _(x):
            @pl.loop(0, size // tile)
            def _(i):
                there = pl.ds(pl.multiple_of(c * size + i * tile, tile), tile)
                ema_out[x, there, :] = (
                    ema_decay * ema_out[x, there, :] + (1.0 - ema_decay) * master_out[x, there, :])

    ahead = min(3, steps)
    for j in range(ahead):
        to_chips(j)
    for j in range(steps):
        if j + ahead < steps:
            to_chips(j + ahead)
        to_holder(j)

    for copy in states:
        copy.wait()
    for c in range(chunks):
        to_hosts(c)

    for j in range(steps):
        for r in range(chips):
            pairs[j, r].wait_send()
        for r in range(chips - 1):
            parts[j, r].wait_send()
        if j in outs:
            outs[j].wait_send()
    for j in range(steps):
        sends[j].wait()


def exchanged(n_e, n_dp, grad, owner_slot, slot_expert, master, one, two, ema):
    rows, cols = grad.shape[0] // n_e, grad.shape[1] // n_dp
    chips = n_dp // CORES
    width = slot_expert.shape[1]
    chunks = CHUNKS
    size = rows // chunks
    steps = chunks * n_e
    dma = pltpu.SemaphoreType.DMA
    half = jnp.bfloat16
    hbm = pl.BlockSpec(memory_space=pl.ANY)
    vmem = pl.BlockSpec(memory_space=pltpu.VMEM)
    smem = pl.BlockSpec(memory_space=pltpu.SMEM)
    return pl.pallas_call(
        functools.partial(exchange_kernel, n_e, n_dp, chunks),
        out_shape=[pltpu.VMEM(master.shape, jnp.float32)] * 4 + [pltpu.VMEM((width, n_e * rows, cols), half)],
        in_specs=[smem, smem] + [hbm] * 5,
        out_specs=[vmem] * 5,
        scratch_shapes=[pltpu.VMEM((n_e, size, cols), half)] * chunks
        + [pltpu.VMEM((n_e, width, size, cols), half)] * chunks
        + [
            pltpu.VMEM((steps, chips, size, cols), half),
            pltpu.VMEM((steps, chips, size, cols), half),
            pltpu.VMEM((steps, chips - 1, size, cols), half),
            pltpu.VMEM((steps, chips - 1, size, cols), half),
            pltpu.VMEM((steps, size, cols), half),
            pltpu.VMEM((n_e, size, cols), half),
            dma((steps, chips)),
            dma((steps, chips)),
            dma((steps, chips)),
            dma((steps, chips - 1)),
            dma((steps, chips - 1)),
            dma((steps,)),
            dma((steps,)),
            dma((4,)),
            dma((steps,)),
            dma((steps,)),
            dma((chunks,)),
        ],
        compiler_params=pltpu.CompilerParams(
            collective_id=0, has_side_effects=True, vmem_limit_bytes=VMEM_LIMIT),
        name="exchange",
    )(owner_slot, slot_expert.reshape(-1), grad, master, one, two, ema)


def per_device(n_e, n_dp, grad_parts, owner_slot, slot_expert, master, moment_one, moment_two, ema_weights):
    return tuple(exchanged(
        n_e, n_dp, grad_parts[0, 0], owner_slot, slot_expert, master, moment_one, moment_two, ema_weights))


def solution(mesh):
    placed = (
        P("dp", "expert", None, None),
        P(),
        P(),
        P(None, "expert", "dp"),
        P(None, "expert", "dp"),
        P(None, "expert", "dp"),
        P(None, "expert", "dp"),
    )
    return jax.shard_map(
        functools.partial(per_device, mesh.shape["expert"], mesh.shape["dp"]),
        mesh=mesh,
        in_specs=placed,
        out_specs=(
            P(None, "expert", "dp"),
            P(None, "expert", "dp"),
            P(None, "expert", "dp"),
            P(None, "expert", "dp"),
            P("expert", None, "dp"),
        ),
        check_vma=False,
    )
```

```python
import functools

import jax
import jax.numpy as jnp
from jax import lax
from jax.experimental import pallas as pl
from jax.experimental.pallas import tpu as pltpu
from jax.sharding import PartitionSpec as P

STEP = 10


beta_one = 0.9
beta_two = 0.999
adam_eps = 1e-08
learn_rate = 0.05
decay_rate = 0.1
ema_decay = 0.99

MESH = pl.DeviceIdType.MESH
CORES = 2
VMEM_LIMIT = 40 * 1024 * 1024
CHUNKS = 2


def row_tile(rows, most):
    return max(t for t in range(16, most + 1, 16) if rows % t == 0)


def adam(gradient, master, one, two):
    scale_one = 1.0 / (1.0 - beta_one**STEP)
    scale_two = 1.0 / (1.0 - beta_two**STEP)
    one_out = beta_one * one + (1.0 - beta_one) * gradient
    two_out = beta_two * two + (1.0 - beta_two) * gradient * gradient
    update = one_out * scale_one / (jnp.sqrt(two_out * scale_two) + adam_eps)
    return master - learn_rate * (update + decay_rate * master), one_out, two_out


def exchange_kernel(n_e, n_dp, chunks, owner, slots, grad, master, one, two, ema,
                    master_out, one_out, two_out, ema_out, replicas, *refs):
    gathered, slotted = refs[:chunks], refs[chunks:2 * chunks]
    (own, got, part, peer, done, held,
     load_sem, pair_send, pair_recv, part_send, part_recv, out_send, out_recv,
     state_sem, slot_send, slot_recv, self_sem) = refs[2 * chunks:]
    chips = n_dp // CORES
    rows = grad.shape[0] // n_e
    cols = grad.shape[1] // n_dp
    size = rows // chunks
    e = lax.axis_index("expert")
    d = lax.axis_index("dp")
    chip, core = d // CORES, d % CORES
    other = 1 - core
    half = n_e // 2
    side, place = e // half, e % half
    tile = row_tile(size, 32)
    steps = chunks * n_e

    barrier = pltpu.get_barrier_semaphore()
    for r in range(1, n_dp):
        pl.semaphore_signal(barrier, inc=1, device_id=(e, lax.rem(d + r, n_dp)), device_id_type=MESH)
    for r in range(1, n_e):
        pl.semaphore_signal(barrier, inc=1, device_id=(lax.rem(e + r, n_e), d), device_id_type=MESH)

    def holder(k):
        if k < half:
            return (1 - side) * half + lax.rem(place + k, half)
        return side * half + lax.rem(place + (k - half + 1), half)

    def block(j, chip_of, core_of):
        first = pl.multiple_of(holder(j % n_e) * rows + (j // n_e) * size, size)
        column = pl.multiple_of((chip_of * CORES + core_of) * cols, cols)
        return grad.at[pl.ds(first, size), pl.ds(column, cols)]

    def chip_at(r):
        return lax.rem(chip + 1 + r, chips)

    loads, pairs = {}, {}
    for j in range(steps):
        for r in range(chips):
            loads[j, r] = pltpu.make_async_copy(block(j, chip_at(r), core), own.at[j, r], load_sem.at[j, r])
            loads[j, r].start()
    pl.semaphore_wait(barrier, n_dp - 1 + n_e - 1)
    for j in range(steps):
        for r in range(chips):
            pairs[j, r] = pltpu.make_async_remote_copy(
                src_ref=block(j, chip_at(r), other), dst_ref=got.at[j, r],
                send_sem=pair_send.at[j, r], recv_sem=pair_recv.at[j, r],
                device_id=(e, chip * CORES + other), device_id_type=MESH)
            pairs[j, r].start()
    states = [pltpu.make_async_copy(src, dst, state_sem.at[i]) for i, (src, dst) in
              enumerate(((master, master_out), (one, one_out), (two, two_out), (ema, ema_out)))]
    for copy in states:
        copy.start()

    parts, outs, sends = {}, {}, {}

    def to_chips(j):
        for r in range(chips - 1):
            loads[j, r].wait()
            pairs[j, r].wait_recv()

            @pl.loop(0, size // tile)
            def _(i):
                at = pl.ds(pl.multiple_of(i * tile, tile), tile)
                total = own[j, r, at, :].astype(jnp.float32) + got[j, r, at, :].astype(jnp.float32)
                part[j, r, at, :] = total.astype(jnp.bfloat16)

            parts[j, r] = pltpu.make_async_remote_copy(
                src_ref=part.at[j, r], dst_ref=peer.at[j, r],
                send_sem=part_send.at[j, r], recv_sem=part_recv.at[j, r],
                device_id=(e, chip_at(r) * CORES + core), device_id_type=MESH)
            parts[j, r].start()

    def to_holder(j):
        c, k = j // n_e, j % n_e
        away = k < n_e - 1
        r_own = chips - 1
        loads[j, r_own].wait()
        pairs[j, r_own].wait_recv()
        for r in range(chips - 1):
            parts[j, r].wait_recv()

        @pl.loop(0, size // tile)
        def _(i):
            at = pl.ds(pl.multiple_of(i * tile, tile), tile)
            total = own[j, r_own, at, :].astype(jnp.float32) + got[j, r_own, at, :].astype(jnp.float32)
            for r in range(chips - 1):
                total = total + peer[j, r, at, :].astype(jnp.float32)
            if away:
                done[j, at, :] = total.astype(jnp.bfloat16)
            else:
                gathered[c][e, at, :] = total.astype(jnp.bfloat16)

        if away:
            outs[j] = pltpu.make_async_remote_copy(
                src_ref=done.at[j], dst_ref=gathered[c].at[e],
                send_sem=out_send.at[j], recv_sem=out_recv.at[j],
                device_id=(holder(k), d), device_id_type=MESH)
            outs[j].start()

    def update(c):
        for k in range(n_e - 1):
            outs[c * n_e + k].wait_recv()

        @pl.loop(0, n_e)
        def _(x):
            position = owner[x]

            @pl.loop(0, size // tile)
            def _(i):
                at = pl.ds(pl.multiple_of(i * tile, tile), tile)
                there = pl.ds(pl.multiple_of(c * size + i * tile, tile), tile)
                gradient = gathered[c][position, at, :].astype(jnp.float32)
                new, first, second = adam(
                    gradient, master_out[x, there, :], one_out[x, there, :], two_out[x, there, :])
                held[x, at, :] = new.astype(jnp.bfloat16)
                master_out[x, there, :] = new
                one_out[x, there, :] = first
                two_out[x, there, :] = second

        width = replicas.shape[0]
        for k in range(n_e):
            host = holder(k)
            for s in range(width):
                wanted = slots[host * width + s]

                @pl.loop(0, size // tile)
                def _(i):
                    at = pl.ds(pl.multiple_of(i * tile, tile), tile)
                    slotted[c][k, s, at, :] = held[wanted, at, :]

    def to_host(j):
        c, k = j // n_e, j % n_e
        first = pl.multiple_of(e * rows + c * size, size)
        target = replicas.at[:, pl.ds(first, size), :]
        if k < n_e - 1:
            sends[j] = pltpu.make_async_remote_copy(
                src_ref=slotted[c].at[k], dst_ref=target,
                send_sem=slot_send.at[j], recv_sem=slot_recv.at[j],
                device_id=(holder(k), d), device_id_type=MESH)
        else:
            sends[j] = pltpu.make_async_copy(slotted[c].at[k], target, self_sem.at[c])
        sends[j].start()

    def average(c):
        @pl.loop(0, n_e)
        def _(x):
            @pl.loop(0, size // tile)
            def _(i):
                there = pl.ds(pl.multiple_of(c * size + i * tile, tile), tile)
                ema_out[x, there, :] = (
                    ema_decay * ema_out[x, there, :] + (1.0 - ema_decay) * master_out[x, there, :])

    ahead = min(3, steps)
    for j in range(ahead):
        to_chips(j)
    for c in range(chunks):
        last = c == chunks - 1
        if c == 0:
            for j in range(n_e):
                to_chips(j + ahead) if j + ahead < steps else None
                to_holder(j)
        if not last:
            for j in range((c + 1) * n_e, (c + 1) * n_e + half):
                to_chips(j + ahead) if j + ahead < steps else None
                to_holder(j)
            for j in range((c + 1) * n_e + half + ahead, min((c + 2) * n_e + ahead, steps)):
                to_chips(j)
        if c == 0:
            for copy in states:
                copy.wait()
        update(c)
        for k in range(n_e):
            to_host(c * n_e + k)
            if not last and k < half:
                to_holder((c + 1) * n_e + half + k)
        average(c)

    for j in range(steps):
        for r in range(chips):
            pairs[j, r].wait_send()
        for r in range(chips - 1):
            parts[j, r].wait_send()
        if j in outs:
            outs[j].wait_send()
    for j in range(steps):
        sends[j].wait()


def exchanged(n_e, n_dp, grad, owner_slot, slot_expert, master, one, two, ema):
    rows, cols = grad.shape[0] // n_e, grad.shape[1] // n_dp
    chips = n_dp // CORES
    width = slot_expert.shape[1]
    chunks = CHUNKS
    size = rows // chunks
    steps = chunks * n_e
    dma = pltpu.SemaphoreType.DMA
    half = jnp.bfloat16
    hbm = pl.BlockSpec(memory_space=pl.ANY)
    vmem = pl.BlockSpec(memory_space=pltpu.VMEM)
    smem = pl.BlockSpec(memory_space=pltpu.SMEM)
    return pl.pallas_call(
        functools.partial(exchange_kernel, n_e, n_dp, chunks),
        out_shape=[pltpu.VMEM(master.shape, jnp.float32)] * 4 + [pltpu.VMEM((width, n_e * rows, cols), half)],
        in_specs=[smem, smem] + [hbm] * 5,
        out_specs=[vmem] * 5,
        scratch_shapes=[pltpu.VMEM((n_e, size, cols), half)] * chunks
        + [pltpu.VMEM((n_e, width, size, cols), half)] * chunks
        + [
            pltpu.VMEM((steps, chips, size, cols), half),
            pltpu.VMEM((steps, chips, size, cols), half),
            pltpu.VMEM((steps, chips - 1, size, cols), half),
            pltpu.VMEM((steps, chips - 1, size, cols), half),
            pltpu.VMEM((steps, size, cols), half),
            pltpu.VMEM((n_e, size, cols), half),
            dma((steps, chips)),
            dma((steps, chips)),
            dma((steps, chips)),
            dma((steps, chips - 1)),
            dma((steps, chips - 1)),
            dma((steps,)),
            dma((steps,)),
            dma((4,)),
            dma((steps,)),
            dma((steps,)),
            dma((chunks,)),
        ],
        compiler_params=pltpu.CompilerParams(
            collective_id=0, has_side_effects=True, vmem_limit_bytes=VMEM_LIMIT),
        name="exchange",
    )(owner_slot, slot_expert.reshape(-1), grad, master, one, two, ema)


def per_device(n_e, n_dp, grad_parts, owner_slot, slot_expert, master, moment_one, moment_two, ema_weights):
    return tuple(exchanged(
        n_e, n_dp, grad_parts[0, 0], owner_slot, slot_expert, master, moment_one, moment_two, ema_weights))


def solution(mesh):
    placed = (
        P("dp", "expert", None, None),
        P(),
        P(),
        P(None, "expert", "dp"),
        P(None, "expert", "dp"),
        P(None, "expert", "dp"),
        P(None, "expert", "dp"),
    )
    return jax.shard_map(
        functools.partial(per_device, mesh.shape["expert"], mesh.shape["dp"]),
        mesh=mesh,
        in_specs=placed,
        out_specs=(
            P(None, "expert", "dp"),
            P(None, "expert", "dp"),
            P(None, "expert", "dp"),
            P(None, "expert", "dp"),
            P("expert", None, "dp"),
        ),
        check_vma=False,
    )
```

```python
import functools

import jax
import jax.numpy as jnp
from jax import lax
from jax.experimental import pallas as pl
from jax.experimental.pallas import tpu as pltpu
from jax.sharding import PartitionSpec as P

STEP = 10


beta_one = 0.9
beta_two = 0.999
adam_eps = 1e-08
learn_rate = 0.05
decay_rate = 0.1
ema_decay = 0.99

MESH = pl.DeviceIdType.MESH
CORES = 2
VMEM_LIMIT = 40 * 1024 * 1024
CHUNKS = 2


def row_tile(rows, most):
    return max(t for t in range(16, most + 1, 16) if rows % t == 0)


def adam(gradient, master, one, two):
    scale_one = 1.0 / (1.0 - beta_one**STEP)
    scale_two = 1.0 / (1.0 - beta_two**STEP)
    one_out = beta_one * one + (1.0 - beta_one) * gradient
    two_out = beta_two * two + (1.0 - beta_two) * gradient * gradient
    update = one_out * scale_one / (jnp.sqrt(two_out * scale_two) + adam_eps)
    return master - learn_rate * (update + decay_rate * master), one_out, two_out


def exchange_kernel(n_e, n_dp, chunks, owner, slots, grad, master, one, two, ema,
                    master_out, one_out, two_out, ema_out, replicas, *refs):
    gathered, slotted = refs[:chunks], refs[chunks:2 * chunks]
    (own, got, part, peer, done, held,
     load_sem, pair_send, pair_recv, part_send, part_recv, out_send, out_recv,
     state_sem, slot_send, slot_recv, self_sem) = refs[2 * chunks:]
    chips = n_dp // CORES
    rows = grad.shape[0] // n_e
    cols = grad.shape[1] // n_dp
    size = rows // chunks
    e = lax.axis_index("expert")
    d = lax.axis_index("dp")
    chip, core = d // CORES, d % CORES
    other = 1 - core
    half = n_e // 2
    side, place = e // half, e % half
    tile = row_tile(size, 32)
    steps = chunks * n_e

    barrier = pltpu.get_barrier_semaphore()
    for r in range(1, n_dp):
        pl.semaphore_signal(barrier, inc=1, device_id=(e, lax.rem(d + r, n_dp)), device_id_type=MESH)
    for r in range(1, n_e):
        pl.semaphore_signal(barrier, inc=1, device_id=(lax.rem(e + r, n_e), d), device_id_type=MESH)

    def holder(k):
        if k == n_e - 1:
            return e
        if k % 2 == 0:
            return (1 - side) * half + lax.rem(place + k // 2, half)
        return side * half + lax.rem(place + k // 2 + 1, half)

    def block(j, chip_of, core_of):
        first = pl.multiple_of(holder(j % n_e) * rows + (j // n_e) * size, size)
        column = pl.multiple_of((chip_of * CORES + core_of) * cols, cols)
        return grad.at[pl.ds(first, size), pl.ds(column, cols)]

    def chip_at(r):
        return lax.rem(chip + 1 + r, chips)

    loads, pairs = {}, {}
    for j in range(steps):
        for r in range(chips):
            loads[j, r] = pltpu.make_async_copy(block(j, chip_at(r), core), own.at[j, r], load_sem.at[j, r])
            loads[j, r].start()
    pl.semaphore_wait(barrier, n_dp - 1 + n_e - 1)
    for j in range(steps):
        for r in range(chips):
            pairs[j, r] = pltpu.make_async_remote_copy(
                src_ref=block(j, chip_at(r), other), dst_ref=got.at[j, r],
                send_sem=pair_send.at[j, r], recv_sem=pair_recv.at[j, r],
                device_id=(e, chip * CORES + other), device_id_type=MESH)
            pairs[j, r].start()
    states = [pltpu.make_async_copy(src, dst, state_sem.at[i]) for i, (src, dst) in
              enumerate(((master, master_out), (one, one_out), (two, two_out), (ema, ema_out)))]
    for copy in states:
        copy.start()

    parts, outs, sends = {}, {}, {}

    def to_chips(j):
        for r in range(chips - 1):
            loads[j, r].wait()
            pairs[j, r].wait_recv()

            @pl.loop(0, size // tile)
            def _(i):
                at = pl.ds(pl.multiple_of(i * tile, tile), tile)
                total = own[j, r, at, :].astype(jnp.float32) + got[j, r, at, :].astype(jnp.float32)
                part[j, r, at, :] = total.astype(jnp.bfloat16)

            parts[j, r] = pltpu.make_async_remote_copy(
                src_ref=part.at[j, r], dst_ref=peer.at[j, r],
                send_sem=part_send.at[j, r], recv_sem=part_recv.at[j, r],
                device_id=(e, chip_at(r) * CORES + core), device_id_type=MESH)
            parts[j, r].start()

    def to_holder(j):
        c, k = j // n_e, j % n_e
        away = k < n_e - 1
        r_own = chips - 1
        loads[j, r_own].wait()
        pairs[j, r_own].wait_recv()
        for r in range(chips - 1):
            parts[j, r].wait_recv()

        @pl.loop(0, size // tile)
        def _(i):
            at = pl.ds(pl.multiple_of(i * tile, tile), tile)
            total = own[j, r_own, at, :].astype(jnp.float32) + got[j, r_own, at, :].astype(jnp.float32)
            for r in range(chips - 1):
                total = total + peer[j, r, at, :].astype(jnp.float32)
            if away:
                done[j, at, :] = total.astype(jnp.bfloat16)
            else:
                gathered[c][e, at, :] = total.astype(jnp.bfloat16)

        if away:
            outs[j] = pltpu.make_async_remote_copy(
                src_ref=done.at[j], dst_ref=gathered[c].at[e],
                send_sem=out_send.at[j], recv_sem=out_recv.at[j],
                device_id=(holder(k), d), device_id_type=MESH)
            outs[j].start()

    def to_hosts(c):
        for k in range(n_e - 1):
            outs[c * n_e + k].wait_recv()

        @pl.loop(0, n_e)
        def _(x):
            position = owner[x]

            @pl.loop(0, size // tile)
            def _(i):
                at = pl.ds(pl.multiple_of(i * tile, tile), tile)
                there = pl.ds(pl.multiple_of(c * size + i * tile, tile), tile)
                gradient = gathered[c][position, at, :].astype(jnp.float32)
                new, first, second = adam(
                    gradient, master_out[x, there, :], one_out[x, there, :], two_out[x, there, :])
                held[x, at, :] = new.astype(jnp.bfloat16)
                master_out[x, there, :] = new
                one_out[x, there, :] = first
                two_out[x, there, :] = second

        width = replicas.shape[0]
        for k in range(n_e):
            host = holder(k)
            for s in range(width):
                wanted = slots[host * width + s]

                @pl.loop(0, size // tile)
                def _(i):
                    at = pl.ds(pl.multiple_of(i * tile, tile), tile)
                    slotted[c][k, s, at, :] = held[wanted, at, :]

            first = pl.multiple_of(e * rows + c * size, size)
            target = replicas.at[:, pl.ds(first, size), :]
            j = c * n_e + k
            if k < n_e - 1:
                sends[j] = pltpu.make_async_remote_copy(
                    src_ref=slotted[c].at[k], dst_ref=target,
                    send_sem=slot_send.at[j], recv_sem=slot_recv.at[j],
                    device_id=(host, d), device_id_type=MESH)
            else:
                sends[j] = pltpu.make_async_copy(slotted[c].at[k], target, self_sem.at[c])
            sends[j].start()

        @pl.loop(0, n_e)
        def _(x):
            @pl.loop(0, size // tile)
            def _(i):
                there = pl.ds(pl.multiple_of(c * size + i * tile, tile), tile)
                ema_out[x, there, :] = (
                    ema_decay * ema_out[x, there, :] + (1.0 - ema_decay) * master_out[x, there, :])

    ahead = min(3, steps)
    for j in range(ahead):
        to_chips(j)
    for j in range(steps):
        if j + ahead < steps:
            to_chips(j + ahead)
        to_holder(j)

    for copy in states:
        copy.wait()
    for c in range(chunks):
        to_hosts(c)

    for j in range(steps):
        for r in range(chips):
            pairs[j, r].wait_send()
        for r in range(chips - 1):
            parts[j, r].wait_send()
        if j in outs:
            outs[j].wait_send()
    for j in range(steps):
        sends[j].wait()


def exchanged(n_e, n_dp, grad, owner_slot, slot_expert, master, one, two, ema):
    rows, cols = grad.shape[0] // n_e, grad.shape[1] // n_dp
    chips = n_dp // CORES
    width = slot_expert.shape[1]
    chunks = CHUNKS
    size = rows // chunks
    steps = chunks * n_e
    dma = pltpu.SemaphoreType.DMA
    half = jnp.bfloat16
    hbm = pl.BlockSpec(memory_space=pl.ANY)
    vmem = pl.BlockSpec(memory_space=pltpu.VMEM)
    smem = pl.BlockSpec(memory_space=pltpu.SMEM)
    return pl.pallas_call(
        functools.partial(exchange_kernel, n_e, n_dp, chunks),
        out_shape=[pltpu.VMEM(master.shape, jnp.float32)] * 4 + [pltpu.VMEM((width, n_e * rows, cols), half)],
        in_specs=[smem, smem] + [hbm] * 5,
        out_specs=[vmem] * 5,
        scratch_shapes=[pltpu.VMEM((n_e, size, cols), half)] * chunks
        + [pltpu.VMEM((n_e, width, size, cols), half)] * chunks
        + [
            pltpu.VMEM((steps, chips, size, cols), half),
            pltpu.VMEM((steps, chips, size, cols), half),
            pltpu.VMEM((steps, chips - 1, size, cols), half),
            pltpu.VMEM((steps, chips - 1, size, cols), half),
            pltpu.VMEM((steps, size, cols), half),
            pltpu.VMEM((n_e, size, cols), half),
            dma((steps, chips)),
            dma((steps, chips)),
            dma((steps, chips)),
            dma((steps, chips - 1)),
            dma((steps, chips - 1)),
            dma((steps,)),
            dma((steps,)),
            dma((4,)),
            dma((steps,)),
            dma((steps,)),
            dma((chunks,)),
        ],
        compiler_params=pltpu.CompilerParams(
            collective_id=0, has_side_effects=True, vmem_limit_bytes=VMEM_LIMIT),
        name="exchange",
    )(owner_slot, slot_expert.reshape(-1), grad, master, one, two, ema)


def per_device(n_e, n_dp, grad_parts, owner_slot, slot_expert, master, moment_one, moment_two, ema_weights):
    return tuple(exchanged(
        n_e, n_dp, grad_parts[0, 0], owner_slot, slot_expert, master, moment_one, moment_two, ema_weights))


def solution(mesh):
    placed = (
        P("dp", "expert", None, None),
        P(),
        P(),
        P(None, "expert", "dp"),
        P(None, "expert", "dp"),
        P(None, "expert", "dp"),
        P(None, "expert", "dp"),
    )
    return jax.shard_map(
        functools.partial(per_device, mesh.shape["expert"], mesh.shape["dp"]),
        mesh=mesh,
        in_specs=placed,
        out_specs=(
            P(None, "expert", "dp"),
            P(None, "expert", "dp"),
            P(None, "expert", "dp"),
            P(None, "expert", "dp"),
            P("expert", None, "dp"),
        ),
        check_vma=False,
    )
```
